32 devices in a mesh: gx: 8 (over z, x), gy: 4 (over y, core).
Axes of the slice: x: 2, y: 2, z: 4, core: 2. Of those that a mesh axis runs over, the one named last changes fastest.
Arguments:
- design: float32 [128, 256, 512], P('gx', 'gy'), may hold values from 0 to 1, as said below
- sensitivity: float32 [128, 256, 512], P('gx', 'gy'), may hold values from 0.1 to 10
- solid_mask: int32 [128, 256, 512], P('gx', 'gy'), may hold values 0 or 1
Outputs:
- new_design: float32 [128, 256, 512], P('gx', 'gy')
- objective_grad: float32 [128, 256, 512], P('gx', 'gy')
- multiplier: float32 [], replicated
The draws below stay inside these ranges and needn't reach their ends.
Inputs may be any that keep to these rules, and one draw needn't show every extreme that they name: design densities lie strictly between 0 and 1.
All inputs are finite; a program needn't handle non-finite values. No bound on the sum of `solid_mask` on one device may be relied on, other than what follows from the above.
Results may differ from the reference program's by a relative error of at most 0.0003.
Values sent between devices are 32-bit elements; how exact they have to be, the bound alone decides.
A program may use at most 64 MiB of HBM per device.

```python
import math
import jax
import jax.numpy as jnp
from jax import lax

NZ = 512
RADIUS = 8
DUAL_ITERS = 2
NX = 128
NY = 256


def box_sum(field_in, which_axis):
    return jnp.roll(field_in, 1, which_axis) + field_in + jnp.roll(field_in, -1, which_axis)


def draw_design(key, part):
    across_x = (jnp.arange(NX, dtype=jnp.float32) + 0.5) / NX
    across_y = (jnp.arange(NY, dtype=jnp.float32) + 0.5) / NY
    trend_part = 0.3 * (across_x[:, None, None] + across_y[None, :, None] - 1.0)
    white_noise = jax.random.normal(key, (NX, NY, NZ), jnp.float32)
    amplitude = 0.35
    smooth_part = white_noise
    for which_axis in range(3):
        smooth_part = box_sum(box_sum(smooth_part, which_axis), which_axis)
    smooth_part = smooth_part * 0.012075
    return jnp.clip(0.5 + trend_part + amplitude * smooth_part, 0.01, 0.99)


def with_ends(result, stream_key, smallest, largest):
    shape = result.shape
    index_at = [jax.random.randint(jax.random.fold_in(stream_key, axis), (), 0, shape[axis]) for axis in range(len(shape))]
    result = result.at[tuple(index_at)].set(smallest)
    longest = shape.index(max(shape))
    index_at[longest] = (index_at[longest] + 1) % shape[longest]
    return result.at[tuple(index_at)].set(largest)


def shard_levels(key, shape, split, low, high):
    loudness, own = 1.0, jax.random.fold_in(key, 6)
    for position, shards_of in split:
        steps = jnp.exp(jax.random.uniform(jax.random.fold_in(own, position), (shards_of,), jnp.float32, low / len(split), high / len(split)))
        loudness = loudness * jnp.repeat(steps, shape[position] // shards_of).reshape([-1 if axis == position else 1 for axis in range(len(shape))])
    return loudness


def setup_inputs(seed: int = 0) -> dict:
    splits = jax.random.split(jax.random.key(seed), 4)
    design = draw_design(jax.random.fold_in(splits[3], 71), 0)
    sensitivity = jnp.clip(jnp.exp(math.log(10.0) - 4.6051702 * jax.random.uniform(splits[1], (NX, NY, NZ), jnp.float32) ** shard_levels(splits[1], (NX, NY, NZ), ((0, 8), (1, 4)), -0.2, 0.2)), 0.1, 10.0)
    solid_mask = with_ends((jax.random.randint(splits[2], (NX, NY, NZ), 0, 8) < 1).astype(jnp.int32), jax.random.fold_in(splits[2], 1), 0, 1)
    return {"design": design, "sensitivity": sensitivity, "solid_mask": solid_mask}


beta_value = 4.0
eta_value = 0.5
volume_share = 0.4
move_limit = 0.2
asym_gap = 0.5

def band(count):
    index = jnp.arange(count)
    gap = jnp.abs(index[:, None] - index[None, :])
    return jnp.maximum(RADIUS + 1 - gap, 0).astype(jnp.float32)

def smooth(field, band_x, band_y, band_z):
    high = lax.Precision.HIGHEST
    out = jnp.einsum('abc,ck->abk', field, band_z, precision=high)
    out = jnp.einsum('ia,abk->ibk', band_x, out, precision=high)
    out = jnp.einsum('jb,ibk->ijk', band_y, out, precision=high)
    return out

def dual_point(lam, design, p_zero, q_zero, p_one, q_one, lower, upper):
    low = design - asym_gap
    upp = design + asym_gap
    a_root = jnp.sqrt(p_zero + lam * p_one)
    b_root = jnp.sqrt(q_zero + lam * q_one)
    raw = (a_root * low + b_root * upp) / (a_root + b_root)
    inside = jnp.logical_and(raw > lower, raw < upper).astype(jnp.float32)
    point = jnp.clip(raw, lower, upper)
    value = p_one / (upp - point) + q_one / (point - low)
    moved = (upp - low) * (a_root * q_one / (2.0 * b_root) - b_root * p_one / (2.0 * a_root)) / (a_root + b_root) ** 2
    change = (p_one / (upp - point) ** 2 - q_one / (point - low) ** 2) * inside * moved
    return (point, value, change)

def reference(design, sensitivity, solid_mask):
    band_x = band(NX)
    band_y = band(NY)
    band_z = band(NZ)
    weight_sum = lax.optimization_barrier(jnp.sum(band_x, 1))[:, None, None] * lax.optimization_barrier(jnp.sum(band_y, 1))[None, :, None] * lax.optimization_barrier(jnp.sum(band_z, 1))[None, None, :]
    filtered = smooth(design, band_x, band_y, band_z) / weight_sum
    shifted = jnp.tanh(beta_value * (filtered - eta_value))
    scale = jnp.tanh(beta_value * eta_value) + jnp.tanh(beta_value * (1.0 - eta_value))
    free = (1 - solid_mask).astype(jnp.float32)
    physical = jnp.where(solid_mask == 1, 1.0, (jnp.tanh(beta_value * eta_value) + shifted) / scale)
    slope = beta_value * (1.0 - shifted * shifted) / scale * free
    objective_grad = smooth(-sensitivity * slope / weight_sum, band_x, band_y, band_z)
    volume_grad = smooth(slope / weight_sum, band_x, band_y, band_z)
    p_zero = 0.25 * (1.001 * jnp.maximum(objective_grad, 0.0) + 0.001 * jnp.maximum(-objective_grad, 0.0) + 1e-05)
    q_zero = 0.25 * (0.001 * jnp.maximum(objective_grad, 0.0) + 1.001 * jnp.maximum(-objective_grad, 0.0) + 1e-05)
    p_one = 0.25 * 1.001 * volume_grad * free
    q_one = 0.25 * 0.001 * volume_grad * free
    lower = jnp.maximum(0.0, design - move_limit)
    upper = jnp.minimum(1.0, design + move_limit)
    offset = jnp.mean(physical) - volume_share - jnp.mean((p_one + q_one) / asym_gap)
    lam = jnp.float32(1.0)
    for turn in range(DUAL_ITERS):
        point, value, change = dual_point(lam, design, p_zero, q_zero, p_one, q_one, lower, upper)
        level = jnp.mean(value) + offset
        rate = jnp.mean(change)
        lam = lam * jnp.exp(-level / (lam * rate - 1e-06))
    point, value, change = dual_point(lam, design, p_zero, q_zero, p_one, q_one, lower, upper)
    new_design = jnp.where(solid_mask == 1, design, point)
    return (new_design, objective_grad, lam)
```

```python
import functools
import math

import jax
import jax.numpy as jnp
from jax import lax
from jax.experimental import pallas as pl
from jax.experimental.pallas import tpu as pltpu
from jax.sharding import PartitionSpec as P

RADIUS = 8
DUAL_ITERS = 2
SPAN = RADIUS + 1
MESH = pl.DeviceIdType.MESH

beta_value = 4.0
eta_value = 0.5
volume_share = 0.4
move_limit = 0.2
asym_gap = 0.5
TANH_MID = math.tanh(beta_value * eta_value)
SCALE = math.tanh(beta_value * eta_value) + math.tanh(beta_value * (1.0 - eta_value))


def missing(distance):
    out = jnp.maximum(RADIUS - distance, 0)
    return (out * (out + 1)) // 2


def cover(cell, total):
    return (SPAN * SPAN - missing(cell) - missing(total - 1 - cell)).astype(jnp.float32)


def split2(x):
    hi = x.astype(jnp.bfloat16)
    lo = (x - hi.astype(jnp.float32)).astype(jnp.bfloat16)
    return hi, lo


def filter_x(src, tile, emit):
    count = src.shape[0] - 2 * RADIUS
    load = lambda i: src[i, tile, :]
    box = load(0)
    for k in range(1, SPAN):
        box = box + load(k)
    window = [box]
    for n in range(1, SPAN):
        box = box + (load(n + RADIUS) - load(n - 1))
        window.append(box)
    total = window[0]
    for k in range(1, SPAN):
        total = total + window[k]
    emit(0, total)
    for i in range(1, count):
        n = i + RADIUS
        box = box + (load(n + RADIUS) - load(n - 1))
        total = total + (box - window[i - 1])
        window.append(box)
        emit(i, total)


def triangle(near, far):
    return jnp.maximum(SPAN - jnp.abs(near - far), 0).astype(jnp.float32).astype(jnp.bfloat16)


def filter_y(src, dst, first, group):
    total, wide, depth = src.shape
    ry = wide - 2 * RADIUS
    jj = lax.broadcasted_iota(jnp.int32, (ry, wide), 0)
    bb = lax.broadcasted_iota(jnp.int32, (ry, wide), 1)
    band = triangle(jj + RADIUS, bb)
    band = jnp.concatenate([band, band], 1)

    def body(g, carry):
        for r in range(group):
            row = g * group + r
            both = jnp.concatenate(split2(src[row]), 0)
            dst[first + row] = jnp.dot(band, both, preferred_element_type=jnp.float32)
        return carry

    lax.fori_loop(0, total // group, body, 0)


def gather_edge(src, first, total, lanes, turn, out):
    tiles = src.shape[1] // 8
    per = GROUPS // tiles
    lane = lax.broadcasted_iota(jnp.int32, (8, 128), 1) // 8

    def body(g, carry):
        packed = jnp.zeros((8, 128), jnp.float32)
        for i in range(GROUPS):
            one = src[first + g * per + i // tiles, pl.ds((i % tiles) * 8, 8), lanes]
            if i > 0:
                one = pltpu.roll(one, 8 * i, 1)
            packed = jnp.where(lane == lax.rem(i + turn, GROUPS), one, packed)
        out[g] = packed
        return carry

    lax.fori_loop(0, total // per, body, 0)


def filter_z(buf, first, total, edge, own_start, edge_start, group, post):
    _, ry, half = buf.shape
    tiles = ry // 8
    per = GROUPS // tiles
    kk = own_start + lax.broadcasted_iota(jnp.int32, (half, half), 1)
    cc = own_start + lax.broadcasted_iota(jnp.int32, (half, half), 0)
    band = triangle(cc, kk)
    kk = own_start + lax.broadcasted_iota(jnp.int32, (128, half), 1)
    cc = edge_start + lax.broadcasted_iota(jnp.int32, (128, half), 0)
    cross = triangle(cc, kk)
    weights = jnp.concatenate([band, band, cross, cross], 0)

    def body(g, carry):
        parts = []
        for r in range(group):
            row = g * group + r
            hi, lo = split2(buf[first + row])
            packed = edge[g * (group // per) + r // per]
            cols = []
            for t in range(tiles):
                i = (r % per) * tiles + t
                cols.append(packed if i == 0 else pltpu.roll(packed, 128 - 8 * i, 1))
            ehi, elo = split2(jnp.concatenate(cols, 0))
            parts.append(jnp.concatenate([hi, lo, ehi, elo], 1))
        out = jnp.dot(jnp.concatenate(parts, 0), weights, preferred_element_type=jnp.float32)
        for r in range(group):
            row = g * group + r
            buf[first + row] = post(row, out[r * ry : (r + 1) * ry])
        return carry

    lax.fori_loop(0, total // group, body, 0)


GROUPS = 16
CHUNKS = 4


def kernel(design, sens, mask, new_hbm, obj_hbm, lam_out, dwide, mbuf, sbuf, atall, vtall, otall, vwide, owide, vfull,
           ofull, vback, oback, dother, mother, new_own, new_other, phys_out, edge_out, edge_in, mbox, xbox, ybox,
           bulk_send, bulk_recv, mask_send, mask_recv, sens_send, sens_recv, x_send, x_recv, back_send, back_recv,
           local_sems, out_sems, m_send, m_recv, gx_send, gx_recv, gy_send, gy_recv):
    rows, ry, depth = design.shape
    half = depth // 2
    both = 2 * rows
    tiles = ry // 8
    gx, gy = lax.axis_index("gx"), lax.axis_index("gy")
    nx, ny = lax.axis_size("gx"), lax.axis_size("gy")
    par = lax.rem(gx, 2)
    pair = gx // 2
    partner = gx + 1 - 2 * par
    has_xl, has_xr = gx >= 2, gx < nx - 2
    has_yl, has_yr = gy >= 1, gy < ny - 1
    xl, xr, yl, yr = (gx - 2, gy), (gx + 2, gy), (gx, gy - 1), (gx, gy + 1)
    mate = (partner, gy)

    barrier = pltpu.get_barrier_semaphore()

    def greet(dev):
        pl.semaphore_signal(barrier, inc=1, device_id=dev, device_id_type=MESH)

    for k in range(1, nx):
        greet((lax.rem(gx + k, nx), gy))
    for k in range(1, ny):
        greet((gx, lax.rem(gy + k, ny)))

    own = pl.ds(pl.multiple_of(par * half, 128), half)
    other = pl.ds(pl.multiple_of((1 - par) * half, 128), half)
    my_rows = pl.ds(par * rows, rows)
    mate_rows = pl.ds((1 - par) * rows, rows)
    mid = pl.ds(RADIUS, ry)
    edge_lanes = pl.ds(pl.multiple_of((1 - par) * (half - 128), 128), 128)
    edge_turn = (1 - par) * (GROUPS - 1)
    edge_start = (1 - par) * half + par * (half - 128)

    def local(k, src, dst):
        return pltpu.make_async_copy(src, dst, local_sems.at[k])

    l_des = local(0, design.at[:, :, own], dwide.at[my_rows, mid, :])
    l_mask = local(1, mask.at[:, :, own], mbuf.at[my_rows])
    l_sens = local(2, sens.at[:, :, own], sbuf.at[my_rows])
    l_dother = local(3, design.at[:, :, other], dother)
    l_mother = local(4, mask.at[:, :, other], mother)
    for one in (l_des, l_mask, l_sens, l_dother, l_mother):
        one.start()
    pl.semaphore_wait(barrier, nx + ny - 2)

    def remote(src, dst, send, recv, dev):
        return pltpu.make_async_remote_copy(
            src_ref=src, dst_ref=dst, send_sem=send, recv_sem=recv, device_id=dev, device_id_type=MESH
        )

    def bulk(k, src, dst, dev):
        return remote(src, dst, bulk_send.at[k], bulk_recv.at[k], dev)

    def begin(two, low, high):
        pl.when(high)(lambda: two[0].start())
        pl.when(low)(lambda: two[1].start())

    def finish(two, low, high):
        pl.when(low)(lambda: two[0].wait_recv())
        pl.when(high)(lambda: two[1].wait_recv())

    def sent(two, low, high):
        pl.when(high)(lambda: two[0].wait_send())
        pl.when(low)(lambda: two[1].wait_send())

    def tile_of(j):
        return pl.ds(pl.multiple_of(lax.rem(j + tiles - 1, tiles) * 8, 8), 8)

    def mask_tile(j):
        tile = tile_of(j)
        return remote(mask.at[:, tile, other], mbuf.at[my_rows, tile, :], mask_send.at[j], mask_recv.at[j], mate)

    def sens_tile(j):
        tile = tile_of(j)
        return remote(sens.at[:, tile, other], sbuf.at[my_rows, tile, :], sens_send.at[j], sens_recv.at[j], mate)

    def start_all(make, first, last):
        def body(j, carry):
            make(j).start()
            return carry

        lax.fori_loop(first, last, body, 0)

    def x_pair(k, buf, j):
        tile = tile_of(j)
        up, dn = (2 * k) * tiles + j, (2 * k + 1) * tiles + j
        return (
            remote(buf.at[pl.ds(both, RADIUS), tile, :], buf.at[pl.ds(0, RADIUS), tile, :],
                   x_send.at[up], x_recv.at[up], xr),
            remote(buf.at[pl.ds(RADIUS, RADIUS), tile, :], buf.at[pl.ds(RADIUS + both, RADIUS), tile, :],
                   x_send.at[dn], x_recv.at[dn], xl),
        )

    def y_pair(k, buf, some):
        return (
            bulk(k, buf.at[some, pl.ds(ry, RADIUS), :], buf.at[some, pl.ds(0, RADIUS), :], yr),
            bulk(k + 1, buf.at[some, pl.ds(RADIUS, RADIUS), :], buf.at[some, pl.ds(RADIUS + ry, RADIUS), :], yl),
        )

    every = pl.ds(0, both)
    r_des = bulk(0, design.at[:, :, other], dwide.at[my_rows, mid, :], mate)
    r_des.start()
    y_own = (
        bulk(1, design.at[:, pl.ds(ry - RADIUS, RADIUS), own], dwide.at[my_rows, pl.ds(0, RADIUS), :], yr),
        bulk(2, design.at[:, pl.ds(0, RADIUS), own], dwide.at[my_rows, pl.ds(RADIUS + ry, RADIUS), :], yl),
    )
    begin(y_own, has_yl, has_yr)
    start_all(mask_tile, 0, EARLY_MASK)

    def zero_y(buf):
        zero = jnp.zeros((both, RADIUS, half), jnp.float32)

        @pl.when(jnp.logical_not(has_yl))
        def _():
            buf[:, 0:RADIUS, :] = zero

        @pl.when(jnp.logical_not(has_yr))
        def _():
            buf[:, RADIUS + ry :, :] = zero

    def zero_x(buf):
        zero = jnp.zeros((RADIUS, ry, half), jnp.float32)

        @pl.when(jnp.logical_not(has_xl))
        def _():
            buf[0:RADIUS] = zero

        @pl.when(jnp.logical_not(has_xr))
        def _():
            buf[RADIUS + both :] = zero

    for buf in (dwide, vwide, owide):
        zero_y(buf)
    for buf in (atall, vtall, otall):
        zero_x(buf)
    phys_out[...] = jnp.zeros_like(phys_out)

    def edge_copy(k):
        return bulk(9 + k, edge_out.at[k], edge_in.at[k], mate)

    def send_edge(k, buf, first):
        gather_edge(buf, first, both, edge_lanes, edge_turn, edge_out.at[k])
        edge_copy(k).start()

    def finish_z(k, buf, first, post):
        edge_copy(k).wait_recv()
        filter_z(buf, first, both, edge_in.at[k], par * half, edge_start, 4, post)

    l_des.wait()
    r_des.wait_recv()
    y_mate = y_pair(3, dwide, mate_rows)
    begin(y_mate, has_yl, has_yr)
    finish(y_own, has_yl, has_yr)
    finish(y_mate, has_yl, has_yr)
    filter_y(dwide, atall, RADIUS, 2)
    send_edge(0, atall, RADIUS)
    start_all(mask_tile, EARLY_MASK, tiles)
    start_all(sens_tile, 0, EARLY_SENS)
    finish_z(0, atall, RADIUS, lambda row, out: out)

    def start_x(k, buf):
        def body(j, carry):
            begin(x_pair(k, buf, j), has_xl, has_xr)
            return carry

        lax.fori_loop(0, tiles, body, 0)

    start_x(0, atall)
    l_mask.wait()
    total_x, total_y = rows * nx, ry * ny
    wz = cover(par * half + lax.broadcasted_iota(jnp.int32, (8, half), 1), depth)

    def stage_one(j, carry):
        tile = tile_of(j)
        start = lax.rem(j + tiles - 1, tiles) * 8
        wy = cover(gy * ry + start + lax.broadcasted_iota(jnp.int32, (8, half), 0), total_y)
        wyz = wy * wz
        finish(x_pair(0, atall, j), has_xl, has_xr)
        mask_tile(j).wait_recv()

        def emit(i, value):
            weight = wyz * cover(pair * both + i, total_x)
            inv = 1.0 / weight
            shifted = jnp.tanh(beta_value * (value * inv - eta_value))
            solid = mbuf[i, tile, :]
            free = (1 - solid).astype(jnp.float32)
            phys_out[...] += jnp.where(solid == 1, 1.0, (TANH_MID + shifted) * (1.0 / SCALE))
            vtall[RADIUS + i, tile, :] = (beta_value / SCALE) * (1.0 - shifted * shifted) * free * inv

        filter_x(atall, tile, emit)
        begin(x_pair(1, vtall, j), has_xl, has_xr)
        return carry

    lax.fori_loop(0, tiles, stage_one, 0)

    def x_only(k, src, dst, y_two):
        def body(j, carry):
            tile = tile_of(j)
            into = pl.ds(pl.multiple_of(lax.rem(j + tiles - 1, tiles) * 8 + RADIUS, 8), 8)
            finish(x_pair(k, src, j), has_xl, has_xr)

            def emit(i, value):
                dst[i, into, :] = value

            filter_x(src, tile, emit)
            pl.when(jnp.logical_and(j == 0, has_yr))(lambda: y_two[0].start())
            pl.when(jnp.logical_and(j == 1, has_yl))(lambda: y_two[1].start())
            return carry

        lax.fori_loop(0, tiles, body, 0)

    y_v = y_pair(5, vwide, every)
    x_only(1, vtall, vwide, y_v)
    finish(y_v, has_yl, has_yr)
    filter_y(vwide, vfull, 0, 2)
    send_edge(1, vfull, 0)
    start_all(sens_tile, EARLY_SENS, tiles)
    l_sens.wait()

    def make_o(j, carry):
        tile = tile_of(j)
        sens_tile(j).wait_recv()

        def times(i, inner):
            for r in range(4):
                otall[RADIUS + 4 * i + r, tile, :] = -sbuf[4 * i + r, tile, :] * vtall[RADIUS + 4 * i + r, tile, :]
            return inner

        lax.fori_loop(0, both // 4, times, 0)
        begin(x_pair(2, otall, j), has_xl, has_xr)
        return carry

    lax.fori_loop(0, EARLY_SENS, make_o, 0)
    finish_z(1, vfull, 0, lambda row, out: out * (1 - mbuf[row]).astype(jnp.float32))

    def back(which, c):
        src, dst = ((vfull, vback), (ofull, oback))[which]
        k = which * rows + c
        return remote(src.at[(1 - par) * rows + c], dst.at[c], back_send.at[k], back_recv.at[k], mate)

    todo = [(which, c) for which in range(2) for c in range(rows)]

    def pump(number):
        for _ in range(min(number, len(todo))):
            which, c = todo.pop(0)
            back(which, c).start()

    pump(PUMP[0])
    lax.fori_loop(EARLY_SENS, tiles, make_o, 0)
    y_o = y_pair(7, owide, every)
    x_only(2, otall, owide, y_o)
    finish(y_o, has_yl, has_yr)
    filter_y(owide, ofull, 0, 2)
    send_edge(2, ofull, 0)
    pump(PUMP[1])
    finish_z(2, ofull, 0, lambda row, out: out)
    o_own = pltpu.make_async_copy(ofull.at[my_rows], obj_hbm.at[:, :, own], out_sems.at[0])
    o_own.start()
    pump(PUMP[2])

    def along(turn, coord, size, place, box, send, recv, after):
        for k in range(1, size):
            peer = lax.rem(coord + k, size)
            remote(box.at[turn, coord], box.at[turn, coord], send.at[turn, k], recv.at[turn, coord], place(peer)).start()
        after()
        for k in range(1, size):
            peer = lax.rem(coord + k, size)
            remote(box.at[turn, peer], box.at[turn, peer], send.at[turn, k], recv.at[turn, peer], place(peer)).wait()
        out = box[turn, 0]
        for k in range(1, size):
            out = out + box[turn, k]
        return out

    def all_sum(turn, tile, after):
        mbox[turn, par] = tile
        tile = along(turn, par, 2, lambda peer: (2 * pair + peer, gy), mbox, m_send, m_recv, after)
        xbox[turn, pair] = tile
        tile = along(turn, pair, nx // 2, lambda peer: (2 * peer + par, gy), xbox, gx_send, gx_recv, lambda: None)
        ybox[turn, gy] = tile
        tile = along(turn, gy, ny, lambda peer: (gx, peer), ybox, gy_send, gy_recv, lambda: None)
        return jnp.sum(tile, axis=1, keepdims=True)

    def fold(x):
        out = x[0:8]
        for k in range(1, x.shape[0] // 8):
            out = out + x[8 * k : 8 * (k + 1)]
        res = out[:, 0:128]
        for k in range(1, x.shape[1] // 128):
            res = res + out[:, 128 * k : 128 * (k + 1)]
        return res

    def shift_of(lam, grad, swing, cell):
        up = jnp.maximum(grad, 0.0)
        down = jnp.maximum(-grad, 0.0)
        a_two = (0.25 * 1.001) * up + (0.25 * 0.001) * down + 0.25e-05 + lam * ((0.25 * 1.001) * swing)
        b_two = (0.25 * 0.001) * up + (0.25 * 1.001) * down + 0.25e-05 + lam * ((0.25 * 0.001) * swing)
        a_inv, b_inv = lax.rsqrt(a_two), lax.rsqrt(b_two)
        a_root, b_root = a_two * a_inv, b_two * b_inv
        inv = pl.reciprocal(a_root + b_root)
        raw = (0.5 * (b_root - a_root)) * inv
        low = jnp.maximum(-cell, -move_limit)
        high = jnp.minimum(1.0 - cell, move_limit)
        return a_root, b_root, a_inv, b_inv, inv, raw, low, high

    part = 32 if ry % 32 == 0 else 8
    pieces = ry // part

    def dual_pass(lam, first, begin_at, end_at, start):
        def body(n, carry):
            i = n // pieces
            at = pl.multiple_of(lax.rem(n, pieces) * part, 8)
            ys, ds = pl.ds(at, part), pl.ds(RADIUS + at, part)
            swing = vfull[i, ys, :]
            a_root, b_root, a_inv, b_inv, inv, raw, low, high = shift_of(lam, ofull[i, ys, :], swing, dwide[i, ds, :])
            point = jnp.clip(raw, low, high)
            p_one, q_one = (0.25 * 1.001) * swing, (0.25 * 0.001) * swing
            recip = pl.reciprocal(asym_gap * asym_gap - point * point)
            r_up, r_low = (asym_gap + point) * recip, (asym_gap - point) * recip
            value_p, value_q = p_one * r_up, q_one * r_low
            moved = 0.5 * (a_root * b_inv * q_one - b_root * a_inv * p_one) * (inv * inv)
            change = jnp.where(
                jnp.logical_and(raw > low, raw < high), (value_p * r_up - value_q * r_low) * moved, 0.0
            )
            out = (carry[0] + fold(value_p + value_q), carry[1] + fold(change))
            if first:
                out = out + (carry[2] + fold(swing),)
            return out

        return lax.fori_loop(begin_at * pieces, end_at * pieces, body, start)

    cells = float(rows * ry * depth)
    cell_count = cells * nx * ny
    index = lax.broadcasted_iota(jnp.int32, (8, 128), 0)

    def pack(parts):
        out = jnp.zeros((8, 128), jnp.float32)
        for k, one in enumerate(parts):
            out = jnp.where(index == k, jnp.sum(one, axis=0, keepdims=True), out)
        return out

    lam = jnp.full((1, 1), 1.0, jnp.float32)
    offset = None
    zero = jnp.zeros((8, 128), jnp.float32)
    span = both // SEGMENTS
    for turn in range(DUAL_ITERS):
        parts = (zero,) * (3 if turn == 0 else 2)
        for seg in range(SEGMENTS):
            parts = dual_pass(lam, turn == 0, seg * span, (seg + 1) * span, parts)
            if seg < SEGMENTS - 1:
                pump(PUMP[3])
        if turn == 0:
            phys = phys_out[:, 0:128]
            for k in range(1, half // 128):
                phys = phys + phys_out[:, 128 * k : 128 * (k + 1)]
            base = parts[2] * (0.25 * (1.001 + 0.001) / asym_gap)
            parts = (parts[0], parts[1], phys - base - volume_share * cells / 1024.0)
        sums = all_sum(turn, pack(parts), lambda: pump(PUMP[4]))
        if turn == 0:
            offset = sums[2:3] / cell_count
        level = sums[0:1] / cell_count + offset
        rate = sums[1:2] / cell_count
        lam = lam * jnp.exp(-level / (lam * rate - 1e-06))
    pump(len(todo))
    lam_out[0, 0] = lam[0, 0]

    def settle(lam, grad, swing, cell, solid):
        raw, low, high = shift_of(lam, grad, swing, cell)[5:]
        return jnp.where(solid == 1, cell, cell + jnp.clip(raw, low, high))

    chunks = CHUNKS if rows % CHUNKS == 0 else 1
    step = rows // chunks

    def leave(k, src, dst, lanes, c):
        some = pl.ds(c * step, step)
        return pltpu.make_async_copy(src.at[some], dst.at[some, :, lanes], out_sems.at[1 + k * chunks + c])

    def last_own(i, carry):
        row = par * rows + i
        new_own[i] = settle(lam, ofull[row], vfull[row], dwide[row, mid, :], mbuf[row])
        return carry

    for c in range(chunks):
        lax.fori_loop(c * step, (c + 1) * step, last_own, 0)
        leave(0, new_own, new_hbm, own, c).start()

    def arrived(c, carry):
        back(0, c).wait_recv()
        return carry

    lax.fori_loop(0, rows, arrived, 0)
    l_dother.wait()
    l_mother.wait()

    def last_other(i, carry):
        back(1, i).wait_recv()
        new_other[i] = settle(lam, oback[i], vback[i], dother[i], mother[i])
        return carry

    for c in range(chunks):
        lax.fori_loop(c * step, (c + 1) * step, last_other, 0)
        leave(1, oback, obj_hbm, other, c).start()
        leave(2, new_other, new_hbm, other, c).start()

    r_des.wait_send()
    for k in range(3):
        edge_copy(k).wait_send()
    for two in (y_own, y_mate, y_v, y_o):
        sent(two, has_yl, has_yr)

    def tile_sent(j, carry):
        mask_tile(j).wait_send()
        sens_tile(j).wait_send()
        for k, buf in enumerate((atall, vtall, otall)):
            sent(x_pair(k, buf, j), has_xl, has_xr)
        return carry

    lax.fori_loop(0, tiles, tile_sent, 0)

    def piece_sent(c, carry):
        back(0, c).wait_send()
        back(1, c).wait_send()
        return carry

    lax.fori_loop(0, rows, piece_sent, 0)
    o_own.wait()
    for c in range(chunks):
        leave(0, new_own, new_hbm, own, c).wait()
        leave(1, oback, obj_hbm, other, c).wait()
        leave(2, new_other, new_hbm, other, c).wait()


EARLY_MASK = 2
EARLY_SENS = 4
SEGMENTS = 4
PUMP = (3, 2, 2, 1, 5)


def per_device(design, sensitivity, solid_mask):
    rows, ry, depth = design.shape
    half = depth // 2
    both = 2 * rows
    tiles = ry // 8
    nx, ny = lax.axis_size("gx"), lax.axis_size("gy")
    f32 = jnp.float32
    block = (rows, ry, depth)
    wide = (both, ry + 2 * RADIUS, half)
    tall = (both + 2 * RADIUS, ry, half)
    strip = (both, ry, half)
    side = (rows, ry, half)
    edges = (3, both * tiles // GROUPS, 8, 128)
    anywhere = pl.BlockSpec(memory_space=pl.ANY)
    dma = pltpu.SemaphoreType.DMA
    vmem = pltpu.VMEM
    new_design, objective_grad, lam = pl.pallas_call(
        kernel,
        out_shape=(
            jax.ShapeDtypeStruct(block, f32),
            jax.ShapeDtypeStruct(block, f32),
            jax.ShapeDtypeStruct((1, 1), f32),
        ),
        in_specs=[anywhere] * 3,
        out_specs=(anywhere, anywhere, pl.BlockSpec(memory_space=pltpu.SMEM)),
        scratch_shapes=[
            vmem(wide, f32),
            vmem(strip, jnp.int32),
            vmem(strip, f32),
            vmem(tall, f32),
            vmem(tall, f32),
            vmem(tall, f32),
            vmem(wide, f32),
            vmem(wide, f32),
            vmem(strip, f32),
            vmem(strip, f32),
            vmem(side, f32),
            vmem(side, f32),
            vmem(side, f32),
            vmem(side, jnp.int32),
            vmem(side, f32),
            vmem(side, f32),
            vmem((8, half), f32),
            vmem(edges, f32),
            vmem(edges, f32),
            vmem((DUAL_ITERS, 2, 8, 128), f32),
            vmem((DUAL_ITERS, nx // 2, 8, 128), f32),
            vmem((DUAL_ITERS, ny, 8, 128), f32),
            dma((12,)),
            dma((12,)),
            dma((tiles,)),
            dma((tiles,)),
            dma((tiles,)),
            dma((tiles,)),
            dma((6 * tiles,)),
            dma((6 * tiles,)),
            dma((2 * rows,)),
            dma((2 * rows,)),
            dma((5,)),
            dma((1 + 3 * CHUNKS,)),
            dma((DUAL_ITERS, 2)),
            dma((DUAL_ITERS, 2)),
            dma((DUAL_ITERS, nx // 2)),
            dma((DUAL_ITERS, nx // 2)),
            dma((DUAL_ITERS, ny)),
            dma((DUAL_ITERS, ny)),
        ],
        compiler_params=pltpu.CompilerParams(
            collective_id=0, has_side_effects=True, vmem_limit_bytes=56 * 1024 * 1024
        ),
    )(design, sensitivity, solid_mask)
    return new_design, objective_grad, lam.reshape(())


def solution(mesh):
    return jax.shard_map(
        per_device,
        mesh=mesh,
        in_specs=(P("gx", "gy", None), P("gx", "gy", None), P("gx", "gy", None)),
        out_specs=(P("gx", "gy", None), P("gx", "gy", None), P()),
        check_vma=False,
    )
```

```python
import functools
import math

import jax
import jax.numpy as jnp
from jax import lax
from jax.experimental import pallas as pl
from jax.experimental.pallas import tpu as pltpu
from jax.sharding import PartitionSpec as P

RADIUS = 8
DUAL_ITERS = 2
SPAN = RADIUS + 1
MESH = pl.DeviceIdType.MESH

beta_value = 4.0
eta_value = 0.5
volume_share = 0.4
move_limit = 0.2
asym_gap = 0.5
TANH_MID = math.tanh(beta_value * eta_value)
SCALE = math.tanh(beta_value * eta_value) + math.tanh(beta_value * (1.0 - eta_value))


def missing(distance):
    out = jnp.maximum(RADIUS - distance, 0)
    return (out * (out + 1)) // 2


def cover(cell, total):
    return (SPAN * SPAN - missing(cell) - missing(total - 1 - cell)).astype(jnp.float32)


def split2(x):
    hi = x.astype(jnp.bfloat16)
    lo = (x - hi.astype(jnp.float32)).astype(jnp.bfloat16)
    return hi, lo


def filter_x(src, tile, emit):
    count = src.shape[0] - 2 * RADIUS
    load = lambda i: src[i, tile, :]
    box = load(0)
    for k in range(1, SPAN):
        box = box + load(k)
    window = [box]
    for n in range(1, SPAN):
        box = box + (load(n + RADIUS) - load(n - 1))
        window.append(box)
    total = window[0]
    for k in range(1, SPAN):
        total = total + window[k]
    emit(0, total)
    for i in range(1, count):
        n = i + RADIUS
        box = box + (load(n + RADIUS) - load(n - 1))
        total = total + (box - window[i - 1])
        window.append(box)
        emit(i, total)


def triangle(near, far):
    return jnp.maximum(SPAN - jnp.abs(near - far), 0).astype(jnp.float32).astype(jnp.bfloat16)


def filter_y(src, dst, first, group):
    total, wide, depth = src.shape
    ry = wide - 2 * RADIUS
    jj = lax.broadcasted_iota(jnp.int32, (ry, wide), 0)
    bb = lax.broadcasted_iota(jnp.int32, (ry, wide), 1)
    band = triangle(jj + RADIUS, bb)
    band = jnp.concatenate([band, band], 1)

    def body(g, carry):
        for r in range(group):
            row = g * group + r
            both = jnp.concatenate(split2(src[row]), 0)
            dst[first + row] = jnp.dot(band, both, preferred_element_type=jnp.float32)
        return carry

    lax.fori_loop(0, total // group, body, 0)


def gather_edge(src, first, total, lanes, turn, out):
    tiles = src.shape[1] // 8
    per = GROUPS // tiles
    lane = lax.broadcasted_iota(jnp.int32, (8, 128), 1) // 8

    def body(g, carry):
        packed = jnp.zeros((8, 128), jnp.float32)
        for i in range(GROUPS):
            one = src[first + g * per + i // tiles, pl.ds((i % tiles) * 8, 8), lanes]
            if i > 0:
                one = pltpu.roll(one, 8 * i, 1)
            packed = jnp.where(lane == lax.rem(i + turn, GROUPS), one, packed)
        out[g] = packed
        return carry

    lax.fori_loop(0, total // per, body, 0)


def filter_z(buf, first, total, edge, own_start, edge_start, group, post):
    _, ry, half = buf.shape
    tiles = ry // 8
    per = GROUPS // tiles
    kk = own_start + lax.broadcasted_iota(jnp.int32, (half, half), 1)
    cc = own_start + lax.broadcasted_iota(jnp.int32, (half, half), 0)
    band = triangle(cc, kk)
    kk = own_start + lax.broadcasted_iota(jnp.int32, (128, half), 1)
    cc = edge_start + lax.broadcasted_iota(jnp.int32, (128, half), 0)
    cross = triangle(cc, kk)
    weights = jnp.concatenate([band, band, cross, cross], 0)

    def body(g, carry):
        parts = []
        for r in range(group):
            row = g * group + r
            hi, lo = split2(buf[first + row])
            packed = edge[g * (group // per) + r // per]
            cols = []
            for t in range(tiles):
                i = (r % per) * tiles + t
                cols.append(packed if i == 0 else pltpu.roll(packed, 128 - 8 * i, 1))
            ehi, elo = split2(jnp.concatenate(cols, 0))
            parts.append(jnp.concatenate([hi, lo, ehi, elo], 1))
        out = jnp.dot(jnp.concatenate(parts, 0), weights, preferred_element_type=jnp.float32)
        for r in range(group):
            row = g * group + r
            buf[first + row] = post(row, out[r * ry : (r + 1) * ry])
        return carry

    lax.fori_loop(0, total // group, body, 0)


GROUPS = 16
CHUNKS = 4


def kernel(design, sens, mask, new_hbm, obj_hbm, lam_out, dwide, mbuf, sbuf, atall, vtall, otall, vwide, owide, vfull,
           ofull, vback, oback, dother, mother, new_own, new_other, phys_out, edge_out, edge_in, mbox, xbox, ybox,
           bulk_send, bulk_recv, mask_send, mask_recv, sens_send, sens_recv, x_send, x_recv, back_send, back_recv,
           local_sems, out_sems, m_send, m_recv, gx_send, gx_recv, gy_send, gy_recv):
    rows, ry, depth = design.shape
    half = depth // 2
    both = 2 * rows
    tiles = ry // 8
    gx, gy = lax.axis_index("gx"), lax.axis_index("gy")
    nx, ny = lax.axis_size("gx"), lax.axis_size("gy")
    par = lax.rem(gx, 2)
    pair = gx // 2
    partner = gx + 1 - 2 * par
    has_xl, has_xr = gx >= 2, gx < nx - 2
    has_yl, has_yr = gy >= 1, gy < ny - 1
    xl, xr, yl, yr = (gx - 2, gy), (gx + 2, gy), (gx, gy - 1), (gx, gy + 1)
    mate = (partner, gy)

    barrier = pltpu.get_barrier_semaphore()

    def greet(dev):
        pl.semaphore_signal(barrier, inc=1, device_id=dev, device_id_type=MESH)

    for k in range(1, nx):
        greet((lax.rem(gx + k, nx), gy))
    for k in range(1, ny):
        greet((gx, lax.rem(gy + k, ny)))

    own = pl.ds(pl.multiple_of(par * half, 128), half)
    other = pl.ds(pl.multiple_of((1 - par) * half, 128), half)
    my_rows = pl.ds(par * rows, rows)
    mate_rows = pl.ds((1 - par) * rows, rows)
    mid = pl.ds(RADIUS, ry)
    edge_lanes = pl.ds(pl.multiple_of((1 - par) * (half - 128), 128), 128)
    edge_turn = (1 - par) * (GROUPS - 1)
    edge_start = (1 - par) * half + par * (half - 128)

    def local(k, src, dst):
        return pltpu.make_async_copy(src, dst, local_sems.at[k])

    l_des = local(0, design.at[:, :, own], dwide.at[my_rows, mid, :])
    l_mask = local(1, mask.at[:, :, own], mbuf.at[my_rows])
    l_sens = local(2, sens.at[:, :, own], sbuf.at[my_rows])
    l_dother = local(3, design.at[:, :, other], dother)
    l_mother = local(4, mask.at[:, :, other], mother)
    for one in (l_des, l_mask, l_sens, l_dother, l_mother):
        one.start()
    pl.semaphore_wait(barrier, nx + ny - 2)

    def remote(src, dst, send, recv, dev):
        return pltpu.make_async_remote_copy(
            src_ref=src, dst_ref=dst, send_sem=send, recv_sem=recv, device_id=dev, device_id_type=MESH
        )

    def bulk(k, src, dst, dev):
        return remote(src, dst, bulk_send.at[k], bulk_recv.at[k], dev)

    def begin(two, low, high):
        pl.when(high)(lambda: two[0].start())
        pl.when(low)(lambda: two[1].start())

    def finish(two, low, high):
        pl.when(low)(lambda: two[0].wait_recv())
        pl.when(high)(lambda: two[1].wait_recv())

    def sent(two, low, high):
        pl.when(high)(lambda: two[0].wait_send())
        pl.when(low)(lambda: two[1].wait_send())

    def tile_of(j):
        return pl.ds(pl.multiple_of(lax.rem(j + tiles - 1, tiles) * 8, 8), 8)

    def mask_tile(j):
        tile = tile_of(j)
        return remote(mask.at[:, tile, other], mbuf.at[my_rows, tile, :], mask_send.at[j], mask_recv.at[j], mate)

    def sens_tile(j):
        tile = tile_of(j)
        return remote(sens.at[:, tile, other], sbuf.at[my_rows, tile, :], sens_send.at[j], sens_recv.at[j], mate)

    def start_all(make, first, last):
        def body(j, carry):
            make(j).start()
            return carry

        lax.fori_loop(first, last, body, 0)

    def x_pair(k, buf, j):
        tile = tile_of(j)
        up, dn = (2 * k) * tiles + j, (2 * k + 1) * tiles + j
        return (
            remote(buf.at[pl.ds(both, RADIUS), tile, :], buf.at[pl.ds(0, RADIUS), tile, :],
                   x_send.at[up], x_recv.at[up], xr),
            remote(buf.at[pl.ds(RADIUS, RADIUS), tile, :], buf.at[pl.ds(RADIUS + both, RADIUS), tile, :],
                   x_send.at[dn], x_recv.at[dn], xl),
        )

    def y_pair(k, buf, some):
        return (
            bulk(k, buf.at[some, pl.ds(ry, RADIUS), :], buf.at[some, pl.ds(0, RADIUS), :], yr),
            bulk(k + 1, buf.at[some, pl.ds(RADIUS, RADIUS), :], buf.at[some, pl.ds(RADIUS + ry, RADIUS), :], yl),
        )

    every = pl.ds(0, both)
    r_des = bulk(0, design.at[:, :, other], dwide.at[my_rows, mid, :], mate)
    r_des.start()
    y_own = (
        bulk(1, design.at[:, pl.ds(ry - RADIUS, RADIUS), own], dwide.at[my_rows, pl.ds(0, RADIUS), :], yr),
        bulk(2, design.at[:, pl.ds(0, RADIUS), own], dwide.at[my_rows, pl.ds(RADIUS + ry, RADIUS), :], yl),
    )
    begin(y_own, has_yl, has_yr)
    start_all(mask_tile, 0, EARLY_MASK)

    def zero_y(buf):
        zero = jnp.zeros((both, RADIUS, half), jnp.float32)

        @pl.when(jnp.logical_not(has_yl))
        def _():
            buf[:, 0:RADIUS, :] = zero

        @pl.when(jnp.logical_not(has_yr))
        def _():
            buf[:, RADIUS + ry :, :] = zero

    def zero_x(buf):
        zero = jnp.zeros((RADIUS, ry, half), jnp.float32)

        @pl.when(jnp.logical_not(has_xl))
        def _():
            buf[0:RADIUS] = zero

        @pl.when(jnp.logical_not(has_xr))
        def _():
            buf[RADIUS + both :] = zero

    for buf in (dwide, vwide, owide):
        zero_y(buf)
    for buf in (atall, vtall, otall):
        zero_x(buf)
    phys_out[...] = jnp.zeros_like(phys_out)

    def edge_copy(k):
        return bulk(9 + k, edge_out.at[k], edge_in.at[k], mate)

    def send_edge(k, buf, first):
        gather_edge(buf, first, both, edge_lanes, edge_turn, edge_out.at[k])
        edge_copy(k).start()

    def finish_z(k, buf, first, post):
        edge_copy(k).wait_recv()
        filter_z(buf, first, both, edge_in.at[k], par * half, edge_start, 8, post)

    l_des.wait()
    r_des.wait_recv()
    y_mate = y_pair(3, dwide, mate_rows)
    begin(y_mate, has_yl, has_yr)
    finish(y_own, has_yl, has_yr)
    finish(y_mate, has_yl, has_yr)
    filter_y(dwide, atall, RADIUS, 8)
    send_edge(0, atall, RADIUS)
    start_all(mask_tile, EARLY_MASK, tiles)
    start_all(sens_tile, 0, EARLY_SENS)
    finish_z(0, atall, RADIUS, lambda row, out: out)

    def start_x(k, buf):
        def body(j, carry):
            begin(x_pair(k, buf, j), has_xl, has_xr)
            return carry

        lax.fori_loop(0, tiles, body, 0)

    start_x(0, atall)
    l_mask.wait()
    total_x, total_y = rows * nx, ry * ny
    wz = cover(par * half + lax.broadcasted_iota(jnp.int32, (8, half), 1), depth)

    def stage_one(j, carry):
        tile = tile_of(j)
        start = lax.rem(j + tiles - 1, tiles) * 8
        wy = cover(gy * ry + start + lax.broadcasted_iota(jnp.int32, (8, half), 0), total_y)
        wyz = wy * wz
        finish(x_pair(0, atall, j), has_xl, has_xr)
        mask_tile(j).wait_recv()

        def emit(i, value):
            weight = wyz * cover(pair * both + i, total_x)
            inv = 1.0 / weight
            shifted = jnp.tanh(beta_value * (value * inv - eta_value))
            solid = mbuf[i, tile, :]
            free = (1 - solid).astype(jnp.float32)
            phys_out[...] += jnp.where(solid == 1, 1.0, (TANH_MID + shifted) * (1.0 / SCALE))
            vtall[RADIUS + i, tile, :] = (beta_value / SCALE) * (1.0 - shifted * shifted) * free * inv

        filter_x(atall, tile, emit)
        begin(x_pair(1, vtall, j), has_xl, has_xr)
        return carry

    lax.fori_loop(0, tiles, stage_one, 0)

    def x_tile(k, src, dst, y_two, j):
        tile = tile_of(j)
        into = pl.ds(pl.multiple_of(lax.rem(j + tiles - 1, tiles) * 8 + RADIUS, 8), 8)
        finish(x_pair(k, src, j), has_xl, has_xr)

        def emit(i, value):
            dst[i, into, :] = value

        filter_x(src, tile, emit)
        pl.when(jnp.logical_and(j == 0, has_yr))(lambda: y_two[0].start())
        pl.when(jnp.logical_and(j == 1, has_yl))(lambda: y_two[1].start())

    def x_only(k, src, dst, y_two, first):
        def body(j, carry):
            x_tile(k, src, dst, y_two, j)
            return carry

        lax.fori_loop(first, tiles, body, 0)

    y_v = y_pair(5, vwide, every)
    x_only(1, vtall, vwide, y_v, 0)
    finish(y_v, has_yl, has_yr)
    filter_y(vwide, vfull, 0, 8)
    send_edge(1, vfull, 0)
    start_all(sens_tile, EARLY_SENS, tiles)
    l_sens.wait()

    def make_o(j, carry):
        tile = tile_of(j)
        sens_tile(j).wait_recv()

        def times(i, inner):
            for r in range(4):
                otall[RADIUS + 4 * i + r, tile, :] = -sbuf[4 * i + r, tile, :] * vtall[RADIUS + 4 * i + r, tile, :]
            return inner

        lax.fori_loop(0, both // 4, times, 0)
        begin(x_pair(2, otall, j), has_xl, has_xr)
        return carry

    lax.fori_loop(0, EARLY_SENS, make_o, 0)
    finish_z(1, vfull, 0, lambda row, out: out * (1 - mbuf[row]).astype(jnp.float32))

    def back(which, c):
        src, dst = ((vfull, vback), (ofull, oback))[which]
        k = which * rows + c
        return remote(src.at[(1 - par) * rows + c], dst.at[c], back_send.at[k], back_recv.at[k], mate)

    todo = [(which, c) for which in range(2) for c in range(rows)]

    def pump(number):
        for _ in range(min(number, len(todo))):
            which, c = todo.pop(0)
            back(which, c).start()

    pump(PUMP[0])
    y_o = y_pair(7, owide, every)

    def o_step(j, carry):
        make_o(j, carry)
        x_tile(2, otall, owide, y_o, j - EARLY_SENS)
        return carry

    lax.fori_loop(EARLY_SENS, tiles, o_step, 0)
    x_only(2, otall, owide, y_o, tiles - EARLY_SENS)
    finish(y_o, has_yl, has_yr)
    filter_y(owide, ofull, 0, 8)
    send_edge(2, ofull, 0)
    pump(PUMP[1])
    finish_z(2, ofull, 0, lambda row, out: out)
    o_own = pltpu.make_async_copy(ofull.at[my_rows], obj_hbm.at[:, :, own], out_sems.at[0])
    o_own.start()
    pump(PUMP[2])

    def along(turn, coord, size, place, box, send, recv, after):
        for k in range(1, size):
            peer = lax.rem(coord + k, size)
            remote(box.at[turn, coord], box.at[turn, coord], send.at[turn, k], recv.at[turn, coord], place(peer)).start()
        after()
        for k in range(1, size):
            peer = lax.rem(coord + k, size)
            remote(box.at[turn, peer], box.at[turn, peer], send.at[turn, k], recv.at[turn, peer], place(peer)).wait()
        out = box[turn, 0]
        for k in range(1, size):
            out = out + box[turn, k]
        return out

    def all_sum(turn, tile, after):
        mbox[turn, par] = tile
        tile = along(turn, par, 2, lambda peer: (2 * pair + peer, gy), mbox, m_send, m_recv, after)
        xbox[turn, pair] = tile
        tile = along(turn, pair, nx // 2, lambda peer: (2 * peer + par, gy), xbox, gx_send, gx_recv, lambda: None)
        ybox[turn, gy] = tile
        tile = along(turn, gy, ny, lambda peer: (gx, peer), ybox, gy_send, gy_recv, lambda: None)
        return jnp.sum(tile, axis=1, keepdims=True)

    def fold(x):
        out = x[0:8]
        for k in range(1, x.shape[0] // 8):
            out = out + x[8 * k : 8 * (k + 1)]
        res = out[:, 0:128]
        for k in range(1, x.shape[1] // 128):
            res = res + out[:, 128 * k : 128 * (k + 1)]
        return res

    def shift_of(lam, grad, swing, cell):
        up = jnp.maximum(grad, 0.0)
        down = jnp.maximum(-grad, 0.0)
        a_two = (0.25 * 1.001) * up + (0.25 * 0.001) * down + 0.25e-05 + lam * ((0.25 * 1.001) * swing)
        b_two = (0.25 * 0.001) * up + (0.25 * 1.001) * down + 0.25e-05 + lam * ((0.25 * 0.001) * swing)
        a_inv, b_inv = lax.rsqrt(a_two), lax.rsqrt(b_two)
        a_root, b_root = a_two * a_inv, b_two * b_inv
        inv = pl.reciprocal(a_root + b_root)
        raw = (0.5 * (b_root - a_root)) * inv
        low = jnp.maximum(-cell, -move_limit)
        high = jnp.minimum(1.0 - cell, move_limit)
        return a_root, b_root, a_inv, b_inv, inv, raw, low, high

    part = 32 if ry % 32 == 0 else 8
    pieces = ry // part

    def dual_pass(lam, first, begin_at, end_at, start):
        def body(n, carry):
            i = n // pieces
            at = pl.multiple_of(lax.rem(n, pieces) * part, 8)
            ys, ds = pl.ds(at, part), pl.ds(RADIUS + at, part)
            swing = vfull[i, ys, :]
            a_root, b_root, a_inv, b_inv, inv, raw, low, high = shift_of(lam, ofull[i, ys, :], swing, dwide[i, ds, :])
            point = jnp.clip(raw, low, high)
            p_one, q_one = (0.25 * 1.001) * swing, (0.25 * 0.001) * swing
            recip = pl.reciprocal(asym_gap * asym_gap - point * point)
            r_up, r_low = (asym_gap + point) * recip, (asym_gap - point) * recip
            value_p, value_q = p_one * r_up, q_one * r_low
            moved = 0.5 * (a_root * b_inv * q_one - b_root * a_inv * p_one) * (inv * inv)
            change = jnp.where(
                jnp.logical_and(raw > low, raw < high), (value_p * r_up - value_q * r_low) * moved, 0.0
            )
            out = (carry[0] + fold(value_p + value_q), carry[1] + fold(change))
            if first:
                out = out + (carry[2] + fold(swing),)
            return out

        return lax.fori_loop(begin_at * pieces, end_at * pieces, body, start)

    cells = float(rows * ry * depth)
    cell_count = cells * nx * ny
    index = lax.broadcasted_iota(jnp.int32, (8, 128), 0)

    def pack(parts):
        out = jnp.zeros((8, 128), jnp.float32)
        for k, one in enumerate(parts):
            out = jnp.where(index == k, jnp.sum(one, axis=0, keepdims=True), out)
        return out

    lam = jnp.full((1, 1), 1.0, jnp.float32)
    offset = None
    zero = jnp.zeros((8, 128), jnp.float32)
    span = both // SEGMENTS
    for turn in range(DUAL_ITERS):
        parts = (zero,) * (3 if turn == 0 else 2)
        for seg in range(SEGMENTS):
            parts = dual_pass(lam, turn == 0, seg * span, (seg + 1) * span, parts)
            if seg < SEGMENTS - 1:
                pump(PUMP[3])
        if turn == 0:
            phys = phys_out[:, 0:128]
            for k in range(1, half // 128):
                phys = phys + phys_out[:, 128 * k : 128 * (k + 1)]
            base = parts[2] * (0.25 * (1.001 + 0.001) / asym_gap)
            parts = (parts[0], parts[1], phys - base - volume_share * cells / 1024.0)
        sums = all_sum(turn, pack(parts), lambda: pump(PUMP[4]))
        if turn == 0:
            offset = sums[2:3] / cell_count
        level = sums[0:1] / cell_count + offset
        rate = sums[1:2] / cell_count
        lam = lam * jnp.exp(-level / (lam * rate - 1e-06))
    pump(len(todo))
    lam_out[0, 0] = lam[0, 0]

    def settle(lam, grad, swing, cell, solid):
        raw, low, high = shift_of(lam, grad, swing, cell)[5:]
        return jnp.where(solid == 1, cell, cell + jnp.clip(raw, low, high))

    chunks = CHUNKS if rows % CHUNKS == 0 else 1
    step = rows // chunks

    def leave(k, src, dst, lanes, c):
        some = pl.ds(c * step, step)
        return pltpu.make_async_copy(src.at[some], dst.at[some, :, lanes], out_sems.at[1 + k * chunks + c])

    def last_own(i, carry):
        row = par * rows + i
        new_own[i] = settle(lam, ofull[row], vfull[row], dwide[row, mid, :], mbuf[row])
        return carry

    for c in range(chunks):
        lax.fori_loop(c * step, (c + 1) * step, last_own, 0)
        leave(0, new_own, new_hbm, own, c).start()

    def arrived(c, carry):
        back(0, c).wait_recv()
        return carry

    lax.fori_loop(0, rows, arrived, 0)
    l_dother.wait()
    l_mother.wait()

    def last_other(i, carry):
        back(1, i).wait_recv()
        new_other[i] = settle(lam, oback[i], vback[i], dother[i], mother[i])
        return carry

    for c in range(chunks):
        lax.fori_loop(c * step, (c + 1) * step, last_other, 0)
        leave(1, oback, obj_hbm, other, c).start()
        leave(2, new_other, new_hbm, other, c).start()

    r_des.wait_send()
    for k in range(3):
        edge_copy(k).wait_send()
    for two in (y_own, y_mate, y_v, y_o):
        sent(two, has_yl, has_yr)

    def tile_sent(j, carry):
        mask_tile(j).wait_send()
        sens_tile(j).wait_send()
        for k, buf in enumerate((atall, vtall, otall)):
            sent(x_pair(k, buf, j), has_xl, has_xr)
        return carry

    lax.fori_loop(0, tiles, tile_sent, 0)

    def piece_sent(c, carry):
        back(0, c).wait_send()
        back(1, c).wait_send()
        return carry

    lax.fori_loop(0, rows, piece_sent, 0)
    o_own.wait()
    for c in range(chunks):
        leave(0, new_own, new_hbm, own, c).wait()
        leave(1, oback, obj_hbm, other, c).wait()
        leave(2, new_other, new_hbm, other, c).wait()


EARLY_MASK = 2
EARLY_SENS = 4
SEGMENTS = 4
PUMP = (7, 4, 2, 1, 7)
VMEM_MIB = 48


def per_device(design, sensitivity, solid_mask):
    rows, ry, depth = design.shape
    half = depth // 2
    both = 2 * rows
    tiles = ry // 8
    nx, ny = lax.axis_size("gx"), lax.axis_size("gy")
    f32 = jnp.float32
    block = (rows, ry, depth)
    wide = (both, ry + 2 * RADIUS, half)
    tall = (both + 2 * RADIUS, ry, half)
    strip = (both, ry, half)
    side = (rows, ry, half)
    edges = (3, both * tiles // GROUPS, 8, 128)
    anywhere = pl.BlockSpec(memory_space=pl.ANY)
    dma = pltpu.SemaphoreType.DMA
    vmem = pltpu.VMEM
    new_design, objective_grad, lam = pl.pallas_call(
        kernel,
        out_shape=(
            jax.ShapeDtypeStruct(block, f32),
            jax.ShapeDtypeStruct(block, f32),
            jax.ShapeDtypeStruct((1, 1), f32),
        ),
        in_specs=[pl.BlockSpec(memory_space=pltpu.HBM)] * 3,
        out_specs=(anywhere, anywhere, pl.BlockSpec(memory_space=pltpu.SMEM)),
        scratch_shapes=[
            vmem(wide, f32),
            vmem(strip, jnp.int32),
            vmem(strip, f32),
            vmem(tall, f32),
            vmem(tall, f32),
            vmem(tall, f32),
            vmem(wide, f32),
            vmem(wide, f32),
            vmem(strip, f32),
            vmem(strip, f32),
            vmem(side, f32),
            vmem(side, f32),
            vmem(side, f32),
            vmem(side, jnp.int32),
            vmem(side, f32),
            vmem(side, f32),
            vmem((8, half), f32),
            vmem(edges, f32),
            vmem(edges, f32),
            vmem((DUAL_ITERS, 2, 8, 128), f32),
            vmem((DUAL_ITERS, nx // 2, 8, 128), f32),
            vmem((DUAL_ITERS, ny, 8, 128), f32),
            dma((12,)),
            dma((12,)),
            dma((tiles,)),
            dma((tiles,)),
            dma((tiles,)),
            dma((tiles,)),
            dma((6 * tiles,)),
            dma((6 * tiles,)),
            dma((2 * rows,)),
            dma((2 * rows,)),
            dma((5,)),
            dma((1 + 3 * CHUNKS,)),
            dma((DUAL_ITERS, 2)),
            dma((DUAL_ITERS, 2)),
            dma((DUAL_ITERS, nx // 2)),
            dma((DUAL_ITERS, nx // 2)),
            dma((DUAL_ITERS, ny)),
            dma((DUAL_ITERS, ny)),
        ],
        compiler_params=pltpu.CompilerParams(
            collective_id=0, has_side_effects=True, vmem_limit_bytes=VMEM_MIB * 1024 * 1024
        ),
    )(design, sensitivity, solid_mask)
    return new_design, objective_grad, lam.reshape(())


def solution(mesh):
    return jax.shard_map(
        per_device,
        mesh=mesh,
        in_specs=(P("gx", "gy", None), P("gx", "gy", None), P("gx", "gy", None)),
        out_specs=(P("gx", "gy", None), P("gx", "gy", None), P()),
        check_vma=False,
    )
```

```python
import functools
import math

import jax
import jax.numpy as jnp
from jax import lax
from jax.experimental import pallas as pl
from jax.experimental.pallas import tpu as pltpu
from jax.sharding import PartitionSpec as P

RADIUS = 8
DUAL_ITERS = 2
SPAN = RADIUS + 1
MESH = pl.DeviceIdType.MESH

beta_value = 4.0
eta_value = 0.5
volume_share = 0.4
move_limit = 0.2
asym_gap = 0.5
TANH_MID = math.tanh(beta_value * eta_value)
SCALE = math.tanh(beta_value * eta_value) + math.tanh(beta_value * (1.0 - eta_value))


def missing(distance):
    out = jnp.maximum(RADIUS - distance, 0)
    return (out * (out + 1)) // 2


def cover(cell, total):
    return (SPAN * SPAN - missing(cell) - missing(total - 1 - cell)).astype(jnp.float32)


def split2(x):
    hi = x.astype(jnp.bfloat16)
    lo = (x - hi.astype(jnp.float32)).astype(jnp.bfloat16)
    return hi, lo


def filter_x(src, tile, emit):
    count = src.shape[0] - 2 * RADIUS
    load = lambda i: src[i, tile, :]
    box = load(0)
    for k in range(1, SPAN):
        box = box + load(k)
    window = [box]
    for n in range(1, SPAN):
        box = box + (load(n + RADIUS) - load(n - 1))
        window.append(box)
    total = window[0]
    for k in range(1, SPAN):
        total = total + window[k]
    emit(0, total)
    for i in range(1, count):
        n = i + RADIUS
        box = box + (load(n + RADIUS) - load(n - 1))
        total = total + (box - window[i - 1])
        window.append(box)
        emit(i, total)


def triangle(near, far):
    return jnp.maximum(SPAN - jnp.abs(near - far), 0).astype(jnp.float32).astype(jnp.bfloat16)


def filter_y(src, dst, first, group):
    total, wide, depth = src.shape
    ry = wide - 2 * RADIUS
    jj = lax.broadcasted_iota(jnp.int32, (ry, wide), 0)
    bb = lax.broadcasted_iota(jnp.int32, (ry, wide), 1)
    band = triangle(jj + RADIUS, bb)
    band = jnp.concatenate([band, band], 1)

    def body(g, carry):
        for r in range(group):
            row = g * group + r
            both = jnp.concatenate(split2(src[row]), 0)
            dst[first + row] = jnp.dot(band, both, preferred_element_type=jnp.float32)
        return carry

    lax.fori_loop(0, total // group, body, 0)


def gather_edge(src, first, total, lanes, turn, out):
    tiles = src.shape[1] // 8
    per = GROUPS // tiles
    lane = lax.broadcasted_iota(jnp.int32, (8, 128), 1) // 8

    def body(g, carry):
        packed = jnp.zeros((8, 128), jnp.float32)
        for i in range(GROUPS):
            one = src[first + g * per + i // tiles, pl.ds((i % tiles) * 8, 8), lanes]
            if i > 0:
                one = pltpu.roll(one, 8 * i, 1)
            packed = jnp.where(lane == lax.rem(i + turn, GROUPS), one, packed)
        out[g] = packed
        return carry

    lax.fori_loop(0, total // per, body, 0)


def filter_z(buf, first, total, edge, own_start, edge_start, group, post):
    _, ry, half = buf.shape
    tiles = ry // 8
    per = GROUPS // tiles
    kk = own_start + lax.broadcasted_iota(jnp.int32, (half, half), 1)
    cc = own_start + lax.broadcasted_iota(jnp.int32, (half, half), 0)
    band = triangle(cc, kk)
    kk = own_start + lax.broadcasted_iota(jnp.int32, (128, half), 1)
    cc = edge_start + lax.broadcasted_iota(jnp.int32, (128, half), 0)
    cross = triangle(cc, kk)
    weights = jnp.concatenate([band, band, cross, cross], 0)

    def body(g, carry):
        parts = []
        for r in range(group):
            row = g * group + r
            hi, lo = split2(buf[first + row])
            packed = edge[g * (group // per) + r // per]
            cols = []
            for t in range(tiles):
                i = (r % per) * tiles + t
                cols.append(packed if i == 0 else pltpu.roll(packed, 128 - 8 * i, 1))
            ehi, elo = split2(jnp.concatenate(cols, 0))
            parts.append(jnp.concatenate([hi, lo, ehi, elo], 1))
        out = jnp.dot(jnp.concatenate(parts, 0), weights, preferred_element_type=jnp.float32)
        for r in range(group):
            row = g * group + r
            buf[first + row] = post(row, out[r * ry : (r + 1) * ry])
        return carry

    lax.fori_loop(0, total // group, body, 0)


GROUPS = 16
CHUNKS = 4


def kernel(design, sens, mask, new_hbm, obj_hbm, lam_out, dwide, mbuf, sbuf, atall, vtall, otall, vwide, owide, vfull,
           ofull, vback, oback, dother, mother, new_own, new_other, phys_out, edge_out, edge_in, mbox, xbox, ybox,
           bulk_send, bulk_recv, mask_send, mask_recv, sens_send, sens_recv, x_send, x_recv, back_send, back_recv,
           local_sems, out_sems, m_send, m_recv, gx_send, gx_recv, gy_send, gy_recv):
    rows, ry, depth = design.shape
    half = depth // 2
    both = 2 * rows
    tiles = ry // 8
    gx, gy = lax.axis_index("gx"), lax.axis_index("gy")
    nx, ny = lax.axis_size("gx"), lax.axis_size("gy")
    par = lax.rem(gx, 2)
    pair = gx // 2
    partner = gx + 1 - 2 * par
    has_xl, has_xr = gx >= 2, gx < nx - 2
    has_yl, has_yr = gy >= 1, gy < ny - 1
    xl, xr, yl, yr = (gx - 2, gy), (gx + 2, gy), (gx, gy - 1), (gx, gy + 1)
    mate = (partner, gy)

    barrier = pltpu.get_barrier_semaphore()

    def greet(dev):
        pl.semaphore_signal(barrier, inc=1, device_id=dev, device_id_type=MESH)

    for k in range(1, nx):
        greet((lax.rem(gx + k, nx), gy))
    for k in range(1, ny):
        greet((gx, lax.rem(gy + k, ny)))

    own = pl.ds(pl.multiple_of(par * half, 128), half)
    other = pl.ds(pl.multiple_of((1 - par) * half, 128), half)
    my_rows = pl.ds(par * rows, rows)
    mate_rows = pl.ds((1 - par) * rows, rows)
    mid = pl.ds(RADIUS, ry)
    edge_lanes = pl.ds(pl.multiple_of((1 - par) * (half - 128), 128), 128)
    edge_turn = (1 - par) * (GROUPS - 1)
    edge_start = (1 - par) * half + par * (half - 128)

    def local(k, src, dst):
        return pltpu.make_async_copy(src, dst, local_sems.at[k])

    l_des = local(0, design.at[:, :, own], dwide.at[my_rows, mid, :])
    l_mask = local(1, mask.at[:, :, own], mbuf.at[my_rows])
    l_sens = local(2, sens.at[:, :, own], sbuf.at[my_rows])
    l_dother = local(3, design.at[:, :, other], dother)
    l_mother = local(4, mask.at[:, :, other], mother)
    for one in (l_des, l_mask, l_sens, l_dother, l_mother):
        one.start()
    pl.semaphore_wait(barrier, nx + ny - 2)

    def remote(src, dst, send, recv, dev):
        return pltpu.make_async_remote_copy(
            src_ref=src, dst_ref=dst, send_sem=send, recv_sem=recv, device_id=dev, device_id_type=MESH
        )

    def bulk(k, src, dst, dev):
        return remote(src, dst, bulk_send.at[k], bulk_recv.at[k], dev)

    def begin(two, low, high):
        pl.when(high)(lambda: two[0].start())
        pl.when(low)(lambda: two[1].start())

    def finish(two, low, high):
        pl.when(low)(lambda: two[0].wait_recv())
        pl.when(high)(lambda: two[1].wait_recv())

    def sent(two, low, high):
        pl.when(high)(lambda: two[0].wait_send())
        pl.when(low)(lambda: two[1].wait_send())

    def tile_of(j):
        return pl.ds(pl.multiple_of(lax.rem(j + tiles - 1, tiles) * 8, 8), 8)

    def mask_tile(j):
        tile = tile_of(j)
        return remote(mask.at[:, tile, other], mbuf.at[my_rows, tile, :], mask_send.at[j], mask_recv.at[j], mate)

    def sens_tile(j):
        tile = tile_of(j)
        return remote(sens.at[:, tile, other], sbuf.at[my_rows, tile, :], sens_send.at[j], sens_recv.at[j], mate)

    def start_all(make, first, last):
        def body(j, carry):
            make(j).start()
            return carry

        lax.fori_loop(first, last, body, 0)

    def x_pair(k, buf, j):
        tile = tile_of(j)
        up, dn = (2 * k) * tiles + j, (2 * k + 1) * tiles + j
        return (
            remote(buf.at[pl.ds(both, RADIUS), tile, :], buf.at[pl.ds(0, RADIUS), tile, :],
                   x_send.at[up], x_recv.at[up], xr),
            remote(buf.at[pl.ds(RADIUS, RADIUS), tile, :], buf.at[pl.ds(RADIUS + both, RADIUS), tile, :],
                   x_send.at[dn], x_recv.at[dn], xl),
        )

    def y_pair(k, buf, some):
        return (
            bulk(k, buf.at[some, pl.ds(ry, RADIUS), :], buf.at[some, pl.ds(0, RADIUS), :], yr),
            bulk(k + 1, buf.at[some, pl.ds(RADIUS, RADIUS), :], buf.at[some, pl.ds(RADIUS + ry, RADIUS), :], yl),
        )

    every = pl.ds(0, both)
    r_des = bulk(0, design.at[:, :, other], dwide.at[my_rows, mid, :], mate)
    r_des.start()
    y_own = (
        bulk(1, design.at[:, pl.ds(ry - RADIUS, RADIUS), own], dwide.at[my_rows, pl.ds(0, RADIUS), :], yr),
        bulk(2, design.at[:, pl.ds(0, RADIUS), own], dwide.at[my_rows, pl.ds(RADIUS + ry, RADIUS), :], yl),
    )
    begin(y_own, has_yl, has_yr)
    start_all(mask_tile, 0, EARLY_MASK)

    def zero_y(buf):
        zero = jnp.zeros((both, RADIUS, half), jnp.float32)

        @pl.when(jnp.logical_not(has_yl))
        def _():
            buf[:, 0:RADIUS, :] = zero

        @pl.when(jnp.logical_not(has_yr))
        def _():
            buf[:, RADIUS + ry :, :] = zero

    def zero_x(buf):
        zero = jnp.zeros((RADIUS, ry, half), jnp.float32)

        @pl.when(jnp.logical_not(has_xl))
        def _():
            buf[0:RADIUS] = zero

        @pl.when(jnp.logical_not(has_xr))
        def _():
            buf[RADIUS + both :] = zero

    for buf in (dwide, vwide, owide):
        zero_y(buf)
    for buf in (atall, vtall, otall):
        zero_x(buf)
    phys_out[...] = jnp.zeros_like(phys_out)

    def edge_copy(k):
        return bulk(9 + k, edge_out.at[k], edge_in.at[k], mate)

    def send_edge(k, buf, first):
        gather_edge(buf, first, both, edge_lanes, edge_turn, edge_out.at[k])
        edge_copy(k).start()

    def finish_z(k, buf, first, post):
        edge_copy(k).wait_recv()
        filter_z(buf, first, both, edge_in.at[k], par * half, edge_start, 8, post)

    l_des.wait()
    r_des.wait_recv()
    y_mate = y_pair(3, dwide, mate_rows)
    begin(y_mate, has_yl, has_yr)
    finish(y_own, has_yl, has_yr)
    finish(y_mate, has_yl, has_yr)
    filter_y(dwide, atall, RADIUS, 8)
    send_edge(0, atall, RADIUS)
    start_all(mask_tile, EARLY_MASK, tiles)
    start_all(sens_tile, 0, EARLY_SENS)
    finish_z(0, atall, RADIUS, lambda row, out: out)

    def start_x(k, buf):
        def body(j, carry):
            begin(x_pair(k, buf, j), has_xl, has_xr)
            return carry

        lax.fori_loop(0, tiles, body, 0)

    start_x(0, atall)
    l_mask.wait()
    total_x, total_y = rows * nx, ry * ny
    wz = cover(par * half + lax.broadcasted_iota(jnp.int32, (8, half), 1), depth)

    def stage_one(j, carry):
        tile = tile_of(j)
        start = lax.rem(j + tiles - 1, tiles) * 8
        wy = cover(gy * ry + start + lax.broadcasted_iota(jnp.int32, (8, half), 0), total_y)
        wyz = wy * wz
        finish(x_pair(0, atall, j), has_xl, has_xr)
        mask_tile(j).wait_recv()

        def emit(i, value):
            weight = wyz * cover(pair * both + i, total_x)
            inv = 1.0 / weight
            shifted = jnp.tanh(beta_value * (value * inv - eta_value))
            solid = mbuf[i, tile, :]
            free = (1 - solid).astype(jnp.float32)
            phys_out[...] += jnp.where(solid == 1, 1.0, (TANH_MID + shifted) * (1.0 / SCALE))
            vtall[RADIUS + i, tile, :] = (beta_value / SCALE) * (1.0 - shifted * shifted) * free * inv

        filter_x(atall, tile, emit)
        begin(x_pair(1, vtall, j), has_xl, has_xr)
        return carry

    lax.fori_loop(0, tiles, stage_one, 0)

    def x_tile(k, src, dst, y_two, j):
        tile = tile_of(j)
        into = pl.ds(pl.multiple_of(lax.rem(j + tiles - 1, tiles) * 8 + RADIUS, 8), 8)
        finish(x_pair(k, src, j), has_xl, has_xr)

        def emit(i, value):
            dst[i, into, :] = value

        filter_x(src, tile, emit)
        pl.when(jnp.logical_and(j == 0, has_yr))(lambda: y_two[0].start())
        pl.when(jnp.logical_and(j == 1, has_yl))(lambda: y_two[1].start())

    def x_only(k, src, dst, y_two, first):
        def body(j, carry):
            x_tile(k, src, dst, y_two, j)
            return carry

        lax.fori_loop(first, tiles, body, 0)

    y_v = y_pair(5, vwide, every)
    x_only(1, vtall, vwide, y_v, 0)
    finish(y_v, has_yl, has_yr)
    filter_y(vwide, vfull, 0, 8)
    send_edge(1, vfull, 0)
    start_all(sens_tile, EARLY_SENS, tiles)
    l_sens.wait()

    def make_o(j, carry):
        tile = tile_of(j)
        sens_tile(j).wait_recv()

        def times(i, inner):
            for r in range(4):
                otall[RADIUS + 4 * i + r, tile, :] = -sbuf[4 * i + r, tile, :] * vtall[RADIUS + 4 * i + r, tile, :]
            return inner

        lax.fori_loop(0, both // 4, times, 0)
        begin(x_pair(2, otall, j), has_xl, has_xr)
        return carry

    y_o = y_pair(7, owide, every)

    def o_step(j, carry):
        make_o(j, carry)
        x_tile(2, otall, owide, y_o, j - LAG)
        return carry

    lax.fori_loop(0, LAG, make_o, 0)
    lax.fori_loop(LAG, EARLY_SENS, o_step, 0)
    finish_z(1, vfull, 0, lambda row, out: out * (1 - mbuf[row]).astype(jnp.float32))

    def back(which, c):
        src, dst = ((vfull, vback), (ofull, oback))[which]
        k = which * rows + c
        return remote(src.at[(1 - par) * rows + c], dst.at[c], back_send.at[k], back_recv.at[k], mate)

    todo = [(which, c) for which in range(2) for c in range(rows)]

    def pump(number):
        for _ in range(min(number, len(todo))):
            which, c = todo.pop(0)
            back(which, c).start()

    pump(PUMP[0])
    lax.fori_loop(EARLY_SENS, tiles, o_step, 0)
    x_only(2, otall, owide, y_o, tiles - LAG)
    finish(y_o, has_yl, has_yr)
    filter_y(owide, ofull, 0, 8)
    send_edge(2, ofull, 0)
    pump(PUMP[1])
    finish_z(2, ofull, 0, lambda row, out: out)
    o_own = pltpu.make_async_copy(ofull.at[my_rows], obj_hbm.at[:, :, own], out_sems.at[0])
    o_own.start()
    pump(PUMP[2])

    def along(turn, coord, size, place, box, send, recv, after):
        for k in range(1, size):
            peer = lax.rem(coord + k, size)
            remote(box.at[turn, coord], box.at[turn, coord], send.at[turn, k], recv.at[turn, coord], place(peer)).start()
        after()
        for k in range(1, size):
            peer = lax.rem(coord + k, size)
            remote(box.at[turn, peer], box.at[turn, peer], send.at[turn, k], recv.at[turn, peer], place(peer)).wait()
        out = box[turn, 0]
        for k in range(1, size):
            out = out + box[turn, k]
        return out

    def all_sum(turn, tile, after):
        mbox[turn, par] = tile
        tile = along(turn, par, 2, lambda peer: (2 * pair + peer, gy), mbox, m_send, m_recv, after)
        xbox[turn, pair] = tile
        tile = along(turn, pair, nx // 2, lambda peer: (2 * peer + par, gy), xbox, gx_send, gx_recv, lambda: None)
        ybox[turn, gy] = tile
        tile = along(turn, gy, ny, lambda peer: (gx, peer), ybox, gy_send, gy_recv, lambda: None)
        return jnp.sum(tile, axis=1, keepdims=True)

    def fold(x):
        out = x[0:8]
        for k in range(1, x.shape[0] // 8):
            out = out + x[8 * k : 8 * (k + 1)]
        res = out[:, 0:128]
        for k in range(1, x.shape[1] // 128):
            res = res + out[:, 128 * k : 128 * (k + 1)]
        return res

    def shift_of(lam, grad, swing, cell):
        up = jnp.maximum(grad, 0.0)
        down = jnp.maximum(-grad, 0.0)
        a_two = (0.25 * 1.001) * up + (0.25 * 0.001) * down + 0.25e-05 + lam * ((0.25 * 1.001) * swing)
        b_two = (0.25 * 0.001) * up + (0.25 * 1.001) * down + 0.25e-05 + lam * ((0.25 * 0.001) * swing)
        a_inv, b_inv = lax.rsqrt(a_two), lax.rsqrt(b_two)
        a_root, b_root = a_two * a_inv, b_two * b_inv
        inv = pl.reciprocal(a_root + b_root)
        raw = (0.5 * (b_root - a_root)) * inv
        low = jnp.maximum(-cell, -move_limit)
        high = jnp.minimum(1.0 - cell, move_limit)
        return a_root, b_root, a_inv, b_inv, inv, raw, low, high

    part = 32 if ry % 32 == 0 else 8
    pieces = ry // part

    def dual_pass(lam, first, begin_at, end_at, start):
        def body(n, carry):
            i = n // pieces
            at = pl.multiple_of(lax.rem(n, pieces) * part, 8)
            ys, ds = pl.ds(at, part), pl.ds(RADIUS + at, part)
            swing = vfull[i, ys, :]
            a_root, b_root, a_inv, b_inv, inv, raw, low, high = shift_of(lam, ofull[i, ys, :], swing, dwide[i, ds, :])
            point = jnp.clip(raw, low, high)
            p_one, q_one = (0.25 * 1.001) * swing, (0.25 * 0.001) * swing
            recip = pl.reciprocal(asym_gap * asym_gap - point * point)
            r_up, r_low = (asym_gap + point) * recip, (asym_gap - point) * recip
            value_p, value_q = p_one * r_up, q_one * r_low
            moved = 0.5 * (a_root * b_inv * q_one - b_root * a_inv * p_one) * (inv * inv)
            change = jnp.where(
                jnp.logical_and(raw > low, raw < high), (value_p * r_up - value_q * r_low) * moved, 0.0
            )
            out = (carry[0] + fold(value_p + value_q), carry[1] + fold(change))
            if first:
                out = out + (carry[2] + fold(swing),)
            return out

        return lax.fori_loop(begin_at * pieces, end_at * pieces, body, start)

    cells = float(rows * ry * depth)
    cell_count = cells * nx * ny
    index = lax.broadcasted_iota(jnp.int32, (8, 128), 0)

    def pack(parts):
        out = jnp.zeros((8, 128), jnp.float32)
        for k, one in enumerate(parts):
            out = jnp.where(index == k, jnp.sum(one, axis=0, keepdims=True), out)
        return out

    lam = jnp.full((1, 1), 1.0, jnp.float32)
    offset = None
    zero = jnp.zeros((8, 128), jnp.float32)
    span = both // SEGMENTS
    for turn in range(DUAL_ITERS):
        parts = (zero,) * (3 if turn == 0 else 2)
        for seg in range(SEGMENTS):
            parts = dual_pass(lam, turn == 0, seg * span, (seg + 1) * span, parts)
            if seg < SEGMENTS - 1:
                pump(PUMP[3])
        if turn == 0:
            phys = phys_out[:, 0:128]
            for k in range(1, half // 128):
                phys = phys + phys_out[:, 128 * k : 128 * (k + 1)]
            base = parts[2] * (0.25 * (1.001 + 0.001) / asym_gap)
            parts = (parts[0], parts[1], phys - base - volume_share * cells / 1024.0)
        sums = all_sum(turn, pack(parts), lambda: pump(PUMP[4]))
        if turn == 0:
            offset = sums[2:3] / cell_count
        level = sums[0:1] / cell_count + offset
        rate = sums[1:2] / cell_count
        lam = lam * jnp.exp(-level / (lam * rate - 1e-06))
    pump(len(todo))
    lam_out[0, 0] = lam[0, 0]

    def settle(lam, grad, swing, cell, solid):
        raw, low, high = shift_of(lam, grad, swing, cell)[5:]
        return jnp.where(solid == 1, cell, cell + jnp.clip(raw, low, high))

    chunks = CHUNKS if rows % CHUNKS == 0 else 1
    step = rows // chunks

    def leave(k, src, dst, lanes, c):
        some = pl.ds(c * step, step)
        return pltpu.make_async_copy(src.at[some], dst.at[some, :, lanes], out_sems.at[1 + k * chunks + c])

    def last_own(i, carry):
        row = par * rows + i
        new_own[i] = settle(lam, ofull[row], vfull[row], dwide[row, mid, :], mbuf[row])
        return carry

    for c in range(chunks):
        lax.fori_loop(c * step, (c + 1) * step, last_own, 0)
        leave(0, new_own, new_hbm, own, c).start()

    def arrived(c, carry):
        back(0, c).wait_recv()
        return carry

    lax.fori_loop(0, rows, arrived, 0)
    l_dother.wait()
    l_mother.wait()

    def last_other(i, carry):
        back(1, i).wait_recv()
        new_other[i] = settle(lam, oback[i], vback[i], dother[i], mother[i])
        return carry

    for c in range(chunks):
        lax.fori_loop(c * step, (c + 1) * step, last_other, 0)
        leave(1, oback, obj_hbm, other, c).start()
        leave(2, new_other, new_hbm, other, c).start()

    r_des.wait_send()
    for k in range(3):
        edge_copy(k).wait_send()
    for two in (y_own, y_mate, y_v, y_o):
        sent(two, has_yl, has_yr)

    def tile_sent(j, carry):
        mask_tile(j).wait_send()
        sens_tile(j).wait_send()
        for k, buf in enumerate((atall, vtall, otall)):
            sent(x_pair(k, buf, j), has_xl, has_xr)
        return carry

    lax.fori_loop(0, tiles, tile_sent, 0)

    def piece_sent(c, carry):
        back(0, c).wait_send()
        back(1, c).wait_send()
        return carry

    lax.fori_loop(0, rows, piece_sent, 0)
    o_own.wait()
    for c in range(chunks):
        leave(0, new_own, new_hbm, own, c).wait()
        leave(1, oback, obj_hbm, other, c).wait()
        leave(2, new_other, new_hbm, other, c).wait()


EARLY_MASK = 3
EARLY_SENS = 6
LAG = 3
SEGMENTS = 4
PUMP = (6, 4, 2, 1, 7)
VMEM_MIB = 48


def per_device(design, sensitivity, solid_mask):
    rows, ry, depth = design.shape
    half = depth // 2
    both = 2 * rows
    tiles = ry // 8
    nx, ny = lax.axis_size("gx"), lax.axis_size("gy")
    f32 = jnp.float32
    block = (rows, ry, depth)
    wide = (both, ry + 2 * RADIUS, half)
    tall = (both + 2 * RADIUS, ry, half)
    strip = (both, ry, half)
    side = (rows, ry, half)
    edges = (3, both * tiles // GROUPS, 8, 128)
    anywhere = pl.BlockSpec(memory_space=pl.ANY)
    dma = pltpu.SemaphoreType.DMA
    vmem = pltpu.VMEM
    new_design, objective_grad, lam = pl.pallas_call(
        kernel,
        out_shape=(
            jax.ShapeDtypeStruct(block, f32),
            jax.ShapeDtypeStruct(block, f32),
            jax.ShapeDtypeStruct((1, 1), f32),
        ),
        in_specs=[pl.BlockSpec(memory_space=pltpu.HBM)] * 3,
        out_specs=(anywhere, anywhere, pl.BlockSpec(memory_space=pltpu.SMEM)),
        scratch_shapes=[
            vmem(wide, f32),
            vmem(strip, jnp.int32),
            vmem(strip, f32),
            vmem(tall, f32),
            vmem(tall, f32),
            vmem(tall, f32),
            vmem(wide, f32),
            vmem(wide, f32),
            vmem(strip, f32),
            vmem(strip, f32),
            vmem(side, f32),
            vmem(side, f32),
            vmem(side, f32),
            vmem(side, jnp.int32),
            vmem(side, f32),
            vmem(side, f32),
            vmem((8, half), f32),
            vmem(edges, f32),
            vmem(edges, f32),
            vmem((DUAL_ITERS, 2, 8, 128), f32),
            vmem((DUAL_ITERS, nx // 2, 8, 128), f32),
            vmem((DUAL_ITERS, ny, 8, 128), f32),
            dma((12,)),
            dma((12,)),
            dma((tiles,)),
            dma((tiles,)),
            dma((tiles,)),
            dma((tiles,)),
            dma((6 * tiles,)),
            dma((6 * tiles,)),
            dma((2 * rows,)),
            dma((2 * rows,)),
            dma((5,)),
            dma((1 + 3 * CHUNKS,)),
            dma((DUAL_ITERS, 2)),
            dma((DUAL_ITERS, 2)),
            dma((DUAL_ITERS, nx // 2)),
            dma((DUAL_ITERS, nx // 2)),
            dma((DUAL_ITERS, ny)),
            dma((DUAL_ITERS, ny)),
        ],
        compiler_params=pltpu.CompilerParams(
            collective_id=0, has_side_effects=True, vmem_limit_bytes=VMEM_MIB * 1024 * 1024
        ),
    )(design, sensitivity, solid_mask)
    return new_design, objective_grad, lam.reshape(())


def solution(mesh):
    return jax.shard_map(
        per_device,
        mesh=mesh,
        in_specs=(P("gx", "gy", None), P("gx", "gy", None), P("gx", "gy", None)),
        out_specs=(P("gx", "gy", None), P("gx", "gy", None), P()),
        check_vma=False,
    )
```
